256 devices in a mesh: rows: 256 (over x, z, y, core).
Axes of the slice: x: 4, y: 4, z: 8, core: 2. Of those that a mesh axis runs over, the one named last changes fastest.
Arguments:
- residual: float32 [131072, 128], P('rows'), may hold values from -6 to 6
- inv_diag: float32 [131072, 512], P('rows'), may hold values from -0.25 to 0.25
- coupling_tiles: float32 [131072, 6, 512], P('rows'), may hold values from -0.0546875 to 0.0546875
- colour: int32 [256], P('rows'), may hold values from 0 to 3, as said below
- tile_cols: int32 [256, 6], P('rows'), may hold values from 0 to 255, as said below
Outputs:
- precond: float32 [131072, 128], P('rows')
The draws below stay inside these ranges and needn't reach their ends.
Inputs may be any that keep to these rules, and one draw needn't show every extreme that they name: Every aligned group of 4 blocks (blocks 4 g to 4 g + 3) holds each colour exactly once. `tile_cols`: row b lists 6 distinct blocks, each within 4 places of b along the cycle of blocks (indices modulo 256), none equal to b and none of b's colour.
All inputs are finite; a program needn't handle non-finite values.
Results may differ from the reference program's by a relative error of at most 0.0001.
Values sent between devices are 32-bit elements; how exact they have to be, the bound alone decides.
A program may use at most 128 MiB of HBM per device.

```python
import jax
import jax.numpy as jnp
from jax import lax

BLOCK = 512
COLS = 128
TILES = 6
COLOURS = 4
REACH = 4
NBLK = 256
NODES = 131072


def colour_and_tiles(key):
    base_key = jax.random.fold_in(key, 11)
    group_keys = jax.random.split(jax.random.fold_in(base_key, 1), NBLK // COLOURS)
    colours = jax.vmap(lambda subkey: jax.random.permutation(subkey, COLOURS))(group_keys).reshape(NBLK).astype(jnp.int32)
    offset_table = jnp.concatenate([jnp.arange(-REACH, 0), jnp.arange(1, REACH + 1)]).astype(jnp.int32)
    blocks = jnp.arange(NBLK, dtype=jnp.int32)
    candidates = (blocks[:, None] + offset_table[None, :]) % NBLK
    same_colour = (colours[candidates] == colours[:, None]).astype(jnp.int32)
    order_keys = jax.random.split(jax.random.fold_in(base_key, 2), NBLK)
    shuffle = jax.vmap(lambda subkey: jax.random.permutation(subkey, 2 * REACH))(order_keys).astype(jnp.int32)
    scores = shuffle + 2 * REACH * same_colour
    picked = jax.lax.top_k(-scores, TILES)[1]
    chosen = jnp.take_along_axis(candidates, picked, axis=1)
    return (colours, chosen.astype(jnp.int32))


def draw_colour(key, part):
    return colour_and_tiles(key)[0]


def draw_tile_cols(key, part):
    return colour_and_tiles(key)[1]


def block_scale(key, extent, pieces, smallest, top_value):
    level, own = 1.0, jax.random.fold_in(key, 6)
    for dim, shards_of in pieces:
        heights = jnp.exp(jax.random.uniform(jax.random.fold_in(own, dim), (shards_of,), jnp.float32, smallest / len(pieces), top_value / len(pieces)))
        level = level * jnp.repeat(heights, extent[dim] // shards_of).reshape([-1 if axis == dim else 1 for axis in range(len(extent))])
    return level


def noise(key, dims, deviation, limit, pieces=(), kind=jnp.bfloat16):
    level = block_scale(key, dims, pieces, -0.22, 0.18) if pieces else 1.0
    array = jax.random.normal(key, dims, jnp.float32) * deviation * level
    return jnp.minimum(jnp.maximum(array, -limit), limit).astype(kind)


def setup_inputs(seed: int = 0) -> dict:
    keys = jax.random.split(jax.random.key(seed), 6)
    return {
        "residual": noise(keys[0], (NODES, COLS), 1.0, 6.0, ((0, 256),), jnp.float32),
        "inv_diag": noise(keys[1], (NODES, BLOCK), BLOCK ** -0.5, 0.25, ((0, 256),), jnp.float32),
        "coupling_tiles": noise(keys[2], (NODES, TILES, BLOCK), (4 * TILES * BLOCK) ** -0.5, 0.0546875, ((0, 256),), jnp.float32),
        "colour": draw_colour(jax.random.fold_in(keys[5], 71), 0),
        "tile_cols": draw_tile_cols(jax.random.fold_in(keys[5], 71), 0),
    }


def relax_colour(current, colour_now, residual, inv_diag, coupling_tiles, colour, tile_cols):
    blocks_x = current.reshape(NBLK, BLOCK, COLS)
    active = jnp.nonzero(colour == colour_now, size=NBLK // COLOURS)[0].astype(jnp.int32)

    def single(block_id):
        first_row = block_id * BLOCK
        couple = lax.dynamic_slice_in_dim(coupling_tiles, first_row, BLOCK, 0).reshape(BLOCK, TILES * BLOCK)
        neighbours = blocks_x[tile_cols[block_id]].reshape(TILES * BLOCK, COLS)
        coupled = jnp.dot(couple, neighbours, precision=lax.Precision.HIGHEST)
        inverse = lax.dynamic_slice_in_dim(inv_diag, first_row, BLOCK, 0)
        rhs_block = lax.dynamic_slice_in_dim(residual, first_row, BLOCK, 0)
        return jnp.dot(inverse, rhs_block - coupled, precision=lax.Precision.HIGHEST)

    updated = lax.map(single, active)
    return blocks_x.at[active].set(updated).reshape(NBLK * BLOCK, COLS)


def reference(residual, inv_diag, coupling_tiles, colour, tile_cols):
    current = jnp.zeros(residual.shape, jnp.float32)
    sweep_order = list(range(COLOURS)) + list(range(COLOURS - 1, -1, -1))
    for colour_now in sweep_order:
        current = relax_colour(current, colour_now, residual, inv_diag, coupling_tiles, colour, tile_cols)
    return current
```

```python
import functools

import jax
import jax.numpy as jnp
from jax import lax
from jax.experimental import pallas as pl
from jax.experimental.pallas import tpu as pltpu
from jax.sharding import PartitionSpec as P

BLOCK = 512
HALF = BLOCK // 2
COLS = 128
TILES = 6
COLOURS = 4
EXCHANGES = 6
WINDOW = 12
CHAINS = 2
NSUB = 1
PIECE = HALF // CHAINS
SUB = PIECE // NSUB
HOPS = (2, -2, 1, -1)
MESH = pl.DeviceIdType.MESH
BF = jnp.bfloat16
F32 = jnp.float32

DUP = len(HOPS)
KINDS = DUP + 5


def split(v):
    hi = v.astype(BF)
    return hi, (v - hi.astype(F32)).astype(BF)


def mm(a, b):
    return jnp.dot(a, b, preferred_element_type=F32)


def swap(v):
    return pltpu.roll(v, COLS // 2, 1)


def left_lanes(rows):
    return lax.broadcasted_iota(jnp.int32, (rows, COLS), 1) < COLS // 2


def kernel(n, colour_ref, tc_ref, res_hbm, inv_hbm, coup_hbm, out_ref,
           res, inv, coup, dsplit, wf, wland, wst, rhs, xin, y, ysend, contrib, tmp, keep_x,
           info, info_smem, tab,
           load_sem, info_send, info_recv, w_send, w_recv, y_sem, x_send, x_recv, smem_sem):
    me = lax.axis_index("rows")
    core = lax.rem(me, 2)
    partner = me + 1 - 2 * core
    pos = lax.rem(me, 4)
    q = lax.rem(me // 2, 2)
    first = me - pos + n - 4
    left = left_lanes(PIECE)

    loads = [
        pltpu.make_async_copy(inv_hbm, inv, load_sem.at[0]),
        pltpu.make_async_copy(res_hbm, res, load_sem.at[1]),
    ]
    for cp in loads:
        cp.start()

    def tile_load(k):
        return pltpu.make_async_copy(coup_hbm.at[k], coup.at[k], load_sem.at[2 + k])

    for k in range(TILES):
        tile_load(k).start()

    others = [4 + lax.rem(pos + r, 4) for r in range(1, 4)] + [0, 1, 2, 3, 8, 9, 10, 11]
    barrier = pltpu.get_barrier_semaphore()
    for t in others:
        pl.semaphore_signal(barrier, inc=1, device_id=(lax.rem(first + t, n),), device_id_type=MESH)

    lane = lax.broadcasted_iota(jnp.int32, (8, 128), 1)
    packed = jnp.where(lane == 0, colour_ref[0], 0)
    for k in range(TILES):
        packed = jnp.where(lane == k + 1, tc_ref[0, k], packed)
    info[4 + pos] = packed

    def pack(v):
        top, bottom = v[0:PIECE], v[PIECE:]
        return jnp.where(left, top, swap(bottom)), jnp.where(left, swap(top), bottom)

    for cp in loads:
        cp.wait()
    dh, dl = split(inv[...])
    dsplit[0:BLOCK] = dh
    dsplit[BLOCK:] = dl
    rh, rl = split(res[...])
    prod = mm(dsplit[...], jnp.concatenate([rh, rl], axis=1))
    prod = prod[0:BLOCK] + prod[BLOCK:]
    prod = prod[:, 0:COLS] + prod[:, COLS:]
    for half in range(2):
        pieces = pack(prod[half * HALF:(half + 1) * HALF])
        for h in range(CHAINS):
            ysend[half, h] = pieces[h]
    y[core] = ysend[core]

    pl.semaphore_wait(barrier, len(others))

    y_copy = pltpu.make_async_remote_copy(
        src_ref=ysend.at[1 - core], dst_ref=y.at[core], send_sem=y_sem.at[0], recv_sem=y_sem.at[1],
        device_id=(partner,), device_id_type=MESH)
    y_copy.start()

    def info_copy(t, slot):
        return pltpu.make_async_remote_copy(
            src_ref=info.at[4 + pos], dst_ref=info.at[slot],
            send_sem=info_send.at[t], recv_sem=info_recv.at[slot],
            device_id=(lax.rem(first + t, n),), device_id_type=MESH)

    def slot_there(t):
        group = t // 4 if isinstance(t, int) else 1
        return 4 * (2 - group) + pos

    for t in others:
        info_copy(t, slot_there(t)).start()

    own_colour = colour_ref[0]

    def active(c):
        return jnp.where(own_colour == c, core, 1 - core)

    def piece(h, par, off, half, j):
        return xin.at[h, par, off, half, pl.ds(j * SUB, SUB)]

    def out_copy(h, par, i, j):
        return pltpu.make_async_remote_copy(
            src_ref=piece(h, par, 2, core, j), dst_ref=piece(h, par, 2 - HOPS[i], core, j),
            send_sem=x_send.at[h, par, i, j], recv_sem=x_recv.at[h, par, i, j],
            device_id=(lax.rem(me + 2 * HOPS[i] + n, n),), device_id_type=MESH)

    def dup(h, par, off, j):
        return pltpu.make_async_remote_copy(
            src_ref=piece(h, par, off, core, j), dst_ref=piece(h, par, off, core, j),
            send_sem=x_send.at[h, par, DUP + off, j], recv_sem=x_recv.at[h, par, DUP + off, j],
            device_id=(partner,), device_id_type=MESH)

    def dup_wait(h, par, off, j):
        pltpu.make_async_remote_copy(
            src_ref=piece(h, par, off, 1 - core, j), dst_ref=piece(h, par, off, 1 - core, j),
            send_sem=x_send.at[h, par, DUP + off, j], recv_sem=x_recv.at[h, par, DUP + off, j],
            device_id=(partner,), device_id_type=MESH).wait_recv()

    def send(h, par):
        for j in range(NSUB):
            for i in range(len(HOPS)):
                out_copy(h, par, i, j).start()
        for j in range(NSUB):
            dup(h, par, 2, j).start()

    y_copy.wait()
    for h in range(CHAINS):
        xin[h, 0, 2, core] = y[active(0), h]
        send(h, 0)

    for c in range(COLOURS):
        for a in range(2):
            for h in range(CHAINS):
                contrib[h, a, c] = jnp.zeros((PIECE, COLS), F32)
    wst[6] = jnp.zeros((BLOCK, BLOCK), BF)
    wst[13] = jnp.zeros((BLOCK, BLOCK), BF)

    def w_copy(k):
        return pltpu.make_async_remote_copy(
            src_ref=wf.at[k, 1 - core], dst_ref=wland.at[k], send_sem=w_send.at[k], recv_sem=w_recv.at[k],
            device_id=(partner,), device_id_type=MESH)

    def premultiply(k, carry):
        tile_load(k).wait()
        ah, al = split(coup[k])
        high = mm(dsplit[...], ah)
        w = high[0:BLOCK] + high[BLOCK:] + mm(dsplit[0:BLOCK], al)
        wf[k, 0] = w[0:HALF]
        wf[k, 1] = w[HALF:]
        w_copy(k).start()
        hi, lo = split(wf[k, core])
        wst[core * 7 + k, 0:HALF] = hi
        wst[core * 7 + k, HALF:] = lo
        return carry

    lax.fori_loop(0, TILES, premultiply, 0)

    for t in others:
        info_copy(t, t).wait_recv()
        info_copy(t, slot_there(t)).wait_send()
    to_smem = pltpu.make_async_copy(info, info_smem, smem_sem)
    to_smem.start()
    to_smem.wait()
    for c in range(COLOURS):
        for sl in range(3):
            where = jnp.int32(0)
            for t in range(1, 4):
                where = jnp.where(info_smem[4 * sl + t, 0, 0] == c, t, where)
            owner = first + 4 * sl + where
            owner = jnp.where(owner >= 2 * n, owner - 2 * n, jnp.where(owner >= n, owner - n, owner))
            off = 2 * (sl - 1) + jnp.where(where >= 2, 1, 0) - q + 2
            off = jnp.where(off < 0, 2, jnp.where(off > 4, 2, off))
            tab[c * 9 + sl] = off
            for a in range(2):
                index = jnp.int32(6)
                slot = 4 + 2 * q + a
                for k in range(TILES):
                    index = jnp.where(info_smem[slot, 0, k + 1] == owner, k, index)
                tab[c * 9 + 3 + 3 * a + sl] = a * 7 + index

    def receive_w(k, carry):
        w_copy(k).wait()
        hi, lo = split(wland[k])
        wst[(1 - core) * 7 + k, 0:HALF] = hi
        wst[(1 - core) * 7 + k, HALF:] = lo
        return carry

    lax.fori_loop(0, TILES, receive_w, 0)

    def colour_of(s):
        return jnp.where(s <= 3, s, 6 - s)

    def make_rhs(h, par, c, sl):
        near, far = ((1, 0), (2, 3 - 2 * q), (3, 4))[sl]
        v = jnp.where(tab[c * 9 + sl] == near, xin[h, par, near], xin[h, par, far])
        for half in range(2):
            hi = v[half].astype(BF).astype(F32)
            lo = v[half] - hi
            row = half * HALF
            rhs[h, sl, row:row + PIECE] = jnp.where(left, hi, swap(lo)).astype(BF)
            rhs[h, sl, row + PIECE:row + HALF] = jnp.where(left, swap(hi), lo).astype(BF)

    def product(h, c, a, sl):
        return mm(wst[tab[c * 9 + 3 + 3 * a + sl]], rhs[h, sl])

    def fold(v):
        v = v[0:HALF] + v[HALF:]
        v = v + swap(v)
        return jnp.where(left, v[0:PIECE], v[PIECE:])

    def relax(h, s):
        par = lax.rem(s, 2)
        c = colour_of(s)
        nxt = active(colour_of(s + 1))
        for i in reversed(range(len(HOPS))):
            for j in range(NSUB):
                out_copy(h, par, i, j).wait_recv()
                dup(h, par, 2 - HOPS[i], j).start()
        base = y[nxt, h]
        for cc in range(COLOURS):
            base = base - jnp.where(c == cc, 0.0, contrib[h, nxt, cc])
        for off in (2, 1, 3):
            for j in range(NSUB):
                dup_wait(h, par, off, j)
        make_rhs(h, par, c, 1)
        acc = product(h, c, nxt, 1)
        for off in (0, 4):
            for j in range(NSUB):
                dup_wait(h, par, off, j)
        make_rhs(h, par, c, 0)
        make_rhs(h, par, c, 2)
        acc = acc + product(h, c, nxt, 0) + product(h, c, nxt, 2)
        mine = fold(acc)
        xin[h, 1 - par, 2, core] = base - mine
        tmp[...] = mine
        for j in range(NSUB):
            for off in range(5):
                dup(h, par, off, j).wait_send()

        @pl.when(s < EXCHANGES - 1)
        def _():
            send(h, 1 - par)

        keep_x[h] = jnp.where(own_colour == c, xin[h, par, 2], keep_x[h])

        @pl.when(s < EXCHANGES - 1)
        def _():
            other = fold(product(h, c, 1 - nxt, 0) + product(h, c, 1 - nxt, 1) + product(h, c, 1 - nxt, 2))
            mine = tmp[...]
            contrib[h, 0, c] = jnp.where(nxt == 0, mine, other)
            contrib[h, 1, c] = jnp.where(nxt == 0, other, mine)

        for j in range(NSUB):
            for i in range(len(HOPS)):
                out_copy(h, par, i, j).wait_send()

    def stage(s, carry):
        for h in range(CHAINS):
            relax(h, s)
        return carry

    keep_x[...] = jnp.zeros_like(keep_x)
    lax.fori_loop(0, EXCHANGES, stage, 0)

    for h in range(CHAINS):
        for j in range(NSUB):
            dup(h, 0, 2, j).start()
    for h in range(CHAINS):
        for j in range(NSUB):
            dup_wait(h, 0, 2, j)
            dup(h, 0, 2, j).wait_send()
    for half in range(2):
        p0, p1 = (jnp.where(own_colour == 0, xin[h, 0, 2, half], keep_x[h, half]) for h in range(CHAINS))
        out_ref[half * HALF:half * HALF + PIECE] = jnp.where(left, p0, swap(p1))
        out_ref[half * HALF + PIECE:(half + 1) * HALF] = jnp.where(left, swap(p0), p1)


def per_device(n, residual, inv_diag, coupling_tiles, colour, tile_cols):
    tiles = jnp.transpose(coupling_tiles, (1, 0, 2))
    smem = pl.BlockSpec(memory_space=pltpu.SMEM)
    hbm = pl.BlockSpec(memory_space=pl.ANY)
    return pl.pallas_call(
        functools.partial(kernel, n),
        out_shape=jax.ShapeDtypeStruct((BLOCK, COLS), F32),
        in_specs=[smem, smem, hbm, hbm, hbm],
        out_specs=pl.BlockSpec(memory_space=pltpu.VMEM),
        scratch_shapes=[
            pltpu.VMEM((BLOCK, COLS), F32),
            pltpu.VMEM((BLOCK, BLOCK), F32),
            pltpu.VMEM((TILES, BLOCK, BLOCK), F32),
            pltpu.VMEM((2 * BLOCK, BLOCK), BF),
            pltpu.VMEM((TILES, 2, HALF, BLOCK), F32),
            pltpu.VMEM((TILES, HALF, BLOCK), F32),
            pltpu.VMEM((14, BLOCK, BLOCK), BF),
            pltpu.VMEM((CHAINS, 3, BLOCK, COLS), BF),
            pltpu.VMEM((CHAINS, 2, 5, 2, PIECE, COLS), F32),
            pltpu.VMEM((2, CHAINS, PIECE, COLS), F32),
            pltpu.VMEM((2, CHAINS, PIECE, COLS), F32),
            pltpu.VMEM((CHAINS, 2, COLOURS, PIECE, COLS), F32),
            pltpu.VMEM((PIECE, COLS), F32),
            pltpu.VMEM((CHAINS, 2, PIECE, COLS), F32),
            pltpu.VMEM((WINDOW, 8, 128), jnp.int32),
            pltpu.SMEM((WINDOW, 8, 128), jnp.int32),
            pltpu.SMEM((9 * COLOURS,), jnp.int32),
            pltpu.SemaphoreType.DMA((2 + TILES,)),
            pltpu.SemaphoreType.DMA((WINDOW,)),
            pltpu.SemaphoreType.DMA((WINDOW,)),
            pltpu.SemaphoreType.DMA((TILES,)),
            pltpu.SemaphoreType.DMA((TILES,)),
            pltpu.SemaphoreType.DMA((2,)),
            pltpu.SemaphoreType.DMA((CHAINS, 2, KINDS, NSUB)),
            pltpu.SemaphoreType.DMA((CHAINS, 2, KINDS, NSUB)),
            pltpu.SemaphoreType.DMA,
        ],
        compiler_params=pltpu.CompilerParams(
            collective_id=0, has_side_effects=True, vmem_limit_bytes=56 * 1024 * 1024),
    )(colour, tile_cols, residual, inv_diag, tiles)


def solution(mesh):
    in_specs = (P("rows", None), P("rows", None), P("rows", None, None), P("rows"), P("rows", None))
    return jax.shard_map(
        functools.partial(per_device, mesh.shape["rows"]), mesh=mesh, in_specs=in_specs,
        out_specs=P("rows", None), check_vma=False)
```

```python
import functools

import jax
import jax.numpy as jnp
from jax import lax
from jax.experimental import pallas as pl
from jax.experimental.pallas import tpu as pltpu
from jax.sharding import PartitionSpec as P

BLOCK = 512
COLS = 128
TILES = 6
COLOURS = 4
EXCHANGES = 6
CHAINS = 2
WIDTH = COLS // 2 // CHAINS
GROUPS = COLS // WIDTH
ROWS = BLOCK // GROUPS
HOPS = (2, -2, 1, -1)
MESH = pl.DeviceIdType.MESH
BF = jnp.bfloat16
F32 = jnp.float32


def split(v):
    hi = v.astype(BF)
    return hi, (v - hi.astype(F32)).astype(BF)


def mm(a, b):
    return jnp.dot(a, b, preferred_element_type=F32)


def turn(v, groups):
    shift = groups * WIDTH % COLS
    return pltpu.roll(v, shift, 1) if shift else v


def kernel(n, colour_ref, tc_ref, res_hbm, inv_hbm, coup_hbm, out_ref,
           res, inv, coup, dsplit, wland, wst, rhs, xin, y, ysend, contrib, tmp, acc, keep, fin,
           info, info_smem, tab,
           load_sem, info_send, info_recv, w_send, w_recv, y_sem, x_send, x_recv, fin_sem):
    me = lax.axis_index("rows")
    core = lax.rem(me, 2)
    partner = me + 1 - 2 * core
    q = lax.rem(me // 2, 2)
    upper = lax.rem(me // 4, 2)
    edge = q == upper

    def chip(hop):
        return lax.rem(me + 2 * hop + n, n)

    pos = lax.rem(me, 4)
    first = me - pos + n - 4
    others = [4 + lax.rem(pos + r, 4) for r in range(1, 4)] + [0, 1, 2, 3, 8, 9, 10, 11]
    barrier = pltpu.get_barrier_semaphore()
    for t in others:
        pl.semaphore_signal(barrier, inc=1, device_id=(lax.rem(first + t, n),), device_id_type=MESH)

    loads = [
        pltpu.make_async_copy(inv_hbm, inv, load_sem.at[0]),
        pltpu.make_async_copy(res_hbm, res, load_sem.at[1]),
    ]
    for cp in loads:
        cp.start()

    def tile_load(k):
        return pltpu.make_async_copy(coup_hbm.at[k], coup.at[k], load_sem.at[2 + k])

    for k in range(TILES):
        tile_load(k).start()

    group = lax.broadcasted_iota(jnp.int32, (ROWS, COLS), 1) // WIDTH

    def pick(values):
        v = values[0]
        for g in range(1, GROUPS):
            v = jnp.where(group == g, values[g], v)
        return v

    for cp in loads:
        cp.wait()
    dh, dl = split(inv[...])
    dsplit[0:BLOCK] = dh
    dsplit[BLOCK:] = dl
    rh, rl = split(res[...])
    prod = mm(dsplit[...], jnp.concatenate([rh, rl], axis=1))
    prod = prod[0:BLOCK] + prod[BLOCK:]
    prod = prod[:, 0:COLS] + prod[:, COLS:]
    for j in range(2):
        for h in range(CHAINS):
            ysend[j, h] = pick([turn(prod[r * ROWS:(r + 1) * ROWS], r - j * CHAINS - h) for r in range(GROUPS)])
    y[core] = ysend[core]

    lane = lax.broadcasted_iota(jnp.int32, (8, 128), 1)
    own_colour = colour_ref[0]
    packed = jnp.where(lane == 0, own_colour, me)
    for k in range(TILES):
        packed = jnp.where(lane == k + 1, tc_ref[0, k], packed)
    info[4 + pos] = packed

    pl.semaphore_wait(barrier, len(others))

    y_copy = pltpu.make_async_remote_copy(
        src_ref=ysend.at[1 - core], dst_ref=y.at[core], send_sem=y_sem.at[0], recv_sem=y_sem.at[1],
        device_id=(partner,), device_id_type=MESH)
    y_copy.start()

    def info_copy(t, slot):
        return pltpu.make_async_remote_copy(
            src_ref=info.at[4 + pos], dst_ref=info.at[slot],
            send_sem=info_send.at[t], recv_sem=info_recv.at[slot],
            device_id=(lax.rem(first + t, n),), device_id_type=MESH)

    def slot_there(t):
        group = t // 4 if isinstance(t, int) else 1
        return 4 * (2 - group) + pos

    for t in others:
        info_copy(t, slot_there(t)).start()

    def w_copy(k):
        return pltpu.make_async_remote_copy(
            src_ref=coup.at[k], dst_ref=wland.at[k], send_sem=w_send.at[k], recv_sem=w_recv.at[k],
            device_id=(partner,), device_id_type=MESH)

    def active(c):
        return jnp.where(own_colour == c, core, 1 - core)

    def out_copy(h, par, i):
        return pltpu.make_async_remote_copy(
            src_ref=xin.at[h, par, 2], dst_ref=xin.at[h, par, 2 - HOPS[i]],
            send_sem=x_send.at[h, par, i], recv_sem=x_recv.at[h, par, i],
            device_id=(chip(HOPS[i]),), device_id_type=MESH)

    def send(h, par):
        for i in range(len(HOPS)):
            out_copy(h, par, i).start()

    y_copy.wait()
    for h in range(CHAINS):
        xin[h, 0, 2] = y[active(0), h]
        send(h, 0)
    def premultiply(k, carry):
        tile_load(k).wait()
        ah, al = split(coup[k])
        left = jnp.concatenate([dsplit[0:BLOCK], dsplit[BLOCK:], dsplit[0:BLOCK]], axis=1)
        coup[k] = mm(left, jnp.concatenate([ah, ah, al], axis=0))
        w_copy(k).start()
        hi, lo = split(coup[k])
        wst[core * 7 + k, 0:BLOCK] = hi
        wst[core * 7 + k, BLOCK:] = lo
        return carry

    lax.fori_loop(0, TILES, premultiply, 0)

    for c in range(COLOURS):
        for a in range(2):
            for h in range(CHAINS):
                contrib[h, a, c] = jnp.zeros((ROWS, COLS), F32)
    wst[6] = jnp.zeros((2 * BLOCK, BLOCK), BF)
    wst[13] = jnp.zeros((2 * BLOCK, BLOCK), BF)
    keep[...] = jnp.zeros_like(keep)

    for t in others:
        info_copy(t, t).wait_recv()
        info_copy(t, slot_there(t)).wait_send()
    to_smem = pltpu.make_async_copy(info, info_smem, load_sem.at[0])
    to_smem.start()
    to_smem.wait()
    for c in range(COLOURS):
        for sl in range(3):
            where = jnp.int32(0)
            for t in range(1, 4):
                where = jnp.where(info_smem[4 * sl + t, 0, 0] == c, t, where)
            owner = first + 4 * sl + where
            owner = jnp.where(owner >= 2 * n, owner - 2 * n, jnp.where(owner >= n, owner - n, owner))
            off = 2 * (sl - 1) + jnp.where(where >= 2, 1, 0) - q + 2
            off = jnp.where(off < 0, 2, jnp.where(off > 4, 2, off))
            tab[c * 9 + sl] = off
            for a in range(2):
                index = jnp.int32(6)
                slot = 4 + 2 * q + a
                for k in range(TILES):
                    index = jnp.where(info_smem[slot, 0, k + 1] == owner, k, index)
                tab[c * 9 + 3 + 3 * a + sl] = a * 7 + index
    block_colour = [info_smem[4 + 2 * q + a, 0, 0] for a in range(2)]

    def receive_w(k, carry):
        w_copy(k).wait()
        hi, lo = split(wland[k])
        wst[(1 - core) * 7 + k, 0:BLOCK] = hi
        wst[(1 - core) * 7 + k, BLOCK:] = lo
        return carry

    lax.fori_loop(0, TILES, receive_w, 0)

    def colour_of(s):
        return jnp.where(s <= 3, s, 6 - s)

    def make_rhs(h, par, c, sl):
        near, far = jnp.maximum(2 * sl - q, 0), jnp.minimum(2 * sl - q + 1, 4)
        v = jnp.where(tab[c * 9 + sl] == near, xin[h, par, near], xin[h, par, far])
        hi = v.astype(BF).astype(F32)
        lo = v - hi
        for r in range(GROUPS):
            rows = pl.ds(pl.multiple_of(sl * BLOCK + r * ROWS, ROWS), ROWS)
            rhs[rows, 0:COLS] = jnp.where(group == r, hi, 0.0).astype(BF)
            rhs[rows, COLS:] = jnp.where(group == r, lo, 0.0).astype(BF)

    def product(c, a, slots):
        tiles = [wst[tab[c * 9 + 3 + 3 * a + sl]] for sl in slots]
        ops = [rhs[pl.ds(pl.multiple_of(sl * BLOCK, BLOCK), BLOCK)] for sl in slots]
        return mm(jnp.concatenate(tiles, axis=1), jnp.concatenate(ops, axis=0))

    def fold(v):
        v = v[0:BLOCK] + v[BLOCK:]
        v = v[:, 0:COLS] + v[:, COLS:]
        rows = [v[r * ROWS:(r + 1) * ROWS] for r in range(GROUPS)]
        total = pick(rows)
        for k in range(1, GROUPS):
            total = total + turn(pick([rows[(g - k) % GROUPS] for g in range(GROUPS)]), -k)
        return total

    def relax(h, s):
        par = lax.rem(s, 2)
        c = colour_of(s)
        nxt = active(colour_of(s + 1))
        base = y[nxt, h]
        for cc in range(COLOURS):
            base = base - jnp.where(c == cc, 0.0, contrib[h, nxt, cc])
        early, late = 2 - 2 * upper, 2 * upper

        def arrived(i):
            pltpu.make_async_remote_copy(
                src_ref=xin.at[h, par, 2], dst_ref=xin.at[h, par, 2],
                send_sem=x_send.at[h, par, i], recv_sem=x_recv.at[h, par, i],
                device_id=(partner,), device_id_type=MESH).wait_recv()

        arrived(3 - upper)
        arrived(1 - upper)

        @pl.when(jnp.logical_not(edge))
        def _():
            arrived(2 + upper)

        make_rhs(h, par, c, 1)
        make_rhs(h, par, c, early)
        acc[...] = base - fold(product(c, nxt, (1, early)))

        @pl.when(edge)
        def _():
            arrived(2 + upper)

        arrived(upper)
        make_rhs(h, par, c, late)
        value = acc[...] - fold(product(c, nxt, (late,)))
        xin[h, 1 - par, 2] = value
        tmp[...] = base - value

        @pl.when(s < EXCHANGES - 1)
        def _():
            send(h, 1 - par)

        for a in range(2):
            keep[a, h] = jnp.where(block_colour[a] == c, xin[h, par, 2], keep[a, h])

        @pl.when(s < EXCHANGES - 1)
        def _():
            other = fold(product(c, 1 - nxt, (0, 1, 2)))
            mine = tmp[...]
            contrib[h, 0, c] = jnp.where(nxt == 0, mine, other)
            contrib[h, 1, c] = jnp.where(nxt == 0, other, mine)

        for i in range(len(HOPS)):
            out_copy(h, par, i).wait_send()

    def stage(s, carry):
        for h in range(CHAINS):
            relax(h, s)
        return carry

    lax.fori_loop(0, EXCHANGES, stage, 0)

    for a in range(2):
        for h in range(CHAINS):
            keep[a, h] = jnp.where(block_colour[a] == 0, xin[h, 0, 2], keep[a, h])
    fin[core] = keep[core]
    fin_copy = pltpu.make_async_remote_copy(
        src_ref=keep.at[1 - core], dst_ref=fin.at[core], send_sem=fin_sem.at[0], recv_sem=fin_sem.at[1],
        device_id=(partner,), device_id_type=MESH)
    fin_copy.start()
    fin_copy.wait()
    for r in range(GROUPS):
        out_ref[r * ROWS:(r + 1) * ROWS] = pick(
            [turn(fin[g // CHAINS, g % CHAINS], g - r) for g in range(GROUPS)])


def per_device(n, residual, inv_diag, coupling_tiles, colour, tile_cols):
    tiles = jnp.transpose(coupling_tiles, (1, 0, 2))
    smem = pl.BlockSpec(memory_space=pltpu.SMEM)
    hbm = pl.BlockSpec(memory_space=pl.ANY)
    return pl.pallas_call(
        functools.partial(kernel, n),
        out_shape=jax.ShapeDtypeStruct((BLOCK, COLS), F32),
        in_specs=[smem, smem, hbm, hbm, hbm],
        out_specs=pl.BlockSpec(memory_space=pltpu.VMEM),
        scratch_shapes=[
            pltpu.VMEM((BLOCK, COLS), F32),
            pltpu.VMEM((BLOCK, BLOCK), F32),
            pltpu.VMEM((TILES, BLOCK, BLOCK), F32),
            pltpu.VMEM((2 * BLOCK, BLOCK), BF),
            pltpu.VMEM((TILES, BLOCK, BLOCK), F32),
            pltpu.VMEM((14, 2 * BLOCK, BLOCK), BF),
            pltpu.VMEM((3 * BLOCK, 2 * COLS), BF),
            pltpu.VMEM((CHAINS, 2, 5, ROWS, COLS), F32),
            pltpu.VMEM((2, CHAINS, ROWS, COLS), F32),
            pltpu.VMEM((2, CHAINS, ROWS, COLS), F32),
            pltpu.VMEM((CHAINS, 2, COLOURS, ROWS, COLS), F32),
            pltpu.VMEM((ROWS, COLS), F32),
            pltpu.VMEM((ROWS, COLS), F32),
            pltpu.VMEM((2, CHAINS, ROWS, COLS), F32),
            pltpu.VMEM((2, CHAINS, ROWS, COLS), F32),
            pltpu.VMEM((12, 8, 128), jnp.int32),
            pltpu.SMEM((12, 8, 128), jnp.int32),
            pltpu.SMEM((9 * COLOURS,), jnp.int32),
            pltpu.SemaphoreType.DMA((2 + TILES,)),
            pltpu.SemaphoreType.DMA((12,)),
            pltpu.SemaphoreType.DMA((12,)),
            pltpu.SemaphoreType.DMA((TILES,)),
            pltpu.SemaphoreType.DMA((TILES,)),
            pltpu.SemaphoreType.DMA((2,)),
            pltpu.SemaphoreType.DMA((CHAINS, 2, len(HOPS))),
            pltpu.SemaphoreType.DMA((CHAINS, 2, len(HOPS))),
            pltpu.SemaphoreType.DMA((2,)),
        ],
        compiler_params=pltpu.CompilerParams(
            collective_id=0, has_side_effects=True, vmem_limit_bytes=56 * 1024 * 1024),
    )(colour, tile_cols, residual, inv_diag, tiles)


def solution(mesh):
    in_specs = (P("rows", None), P("rows", None), P("rows", None, None), P("rows"), P("rows", None))
    return jax.shard_map(
        functools.partial(per_device, mesh.shape["rows"]), mesh=mesh, in_specs=in_specs,
        out_specs=P("rows", None), check_vma=False)
```

```python
import functools

import jax
import jax.numpy as jnp
from jax import lax
from jax.experimental import pallas as pl
from jax.experimental.pallas import tpu as pltpu
from jax.sharding import PartitionSpec as P

BLOCK = 512
COLS = 128
TILES = 6
COLOURS = 4
EXCHANGES = 6
CHAINS = 2
WIDTH = COLS // 2 // CHAINS
GROUPS = COLS // WIDTH
ROWS = BLOCK // GROUPS
HOPS = (2, -2, 1, -1)
MESH = pl.DeviceIdType.MESH
BF = jnp.bfloat16
F32 = jnp.float32


def split(v):
    hi = v.astype(BF)
    return hi, (v - hi.astype(F32)).astype(BF)


def mm(a, b):
    return jnp.dot(a, b, preferred_element_type=F32)


def turn(v, groups):
    shift = groups * WIDTH % COLS
    return pltpu.roll(v, shift, 1) if shift else v


def kernel(n, colour_ref, tc_ref, res_hbm, inv_hbm, coup_hbm, out_ref,
           res, inv, coup, dsplit, wland, wst, rhs, xin, y, ysend, contrib, tmp, acc, keep, fin,
           info, info_smem, tab,
           load_sem, info_send, info_recv, w_send, w_recv, y_sem, x_send, x_recv, fin_sem):
    me = lax.axis_index("rows")
    core = lax.rem(me, 2)
    partner = me + 1 - 2 * core
    q = lax.rem(me // 2, 2)
    upper = lax.rem(me // 4, 2)
    edge = q == upper

    def chip(hop):
        return lax.rem(me + 2 * hop + n, n)

    pos = lax.rem(me, 4)
    first = me - pos + n - 4
    others = [4 + lax.rem(pos + r, 4) for r in range(1, 4)] + [0, 1, 2, 3, 8, 9, 10, 11]
    barrier = pltpu.get_barrier_semaphore()
    for t in others:
        pl.semaphore_signal(barrier, inc=1, device_id=(lax.rem(first + t, n),), device_id_type=MESH)

    loads = [
        pltpu.make_async_copy(inv_hbm, inv, load_sem.at[0]),
        pltpu.make_async_copy(res_hbm, res, load_sem.at[1]),
    ]
    for cp in loads:
        cp.start()

    def tile_load(k):
        return pltpu.make_async_copy(coup_hbm.at[k], coup.at[k], load_sem.at[2 + k])

    for k in range(TILES):
        tile_load(k).start()

    group = lax.broadcasted_iota(jnp.int32, (ROWS, COLS), 1) // WIDTH

    def pick(values):
        v = values[0]
        for g in range(1, GROUPS):
            v = jnp.where(group == g, values[g], v)
        return v

    for cp in loads:
        cp.wait()
    dh, dl = split(inv[...])
    dsplit[0:BLOCK] = dh
    dsplit[BLOCK:] = dl
    rh, rl = split(res[...])
    prod = mm(dsplit[...], jnp.concatenate([rh, rl], axis=1))
    prod = prod[0:BLOCK] + prod[BLOCK:]
    prod = prod[:, 0:COLS] + prod[:, COLS:]
    for j in range(2):
        for h in range(CHAINS):
            ysend[j, h] = pick([turn(prod[r * ROWS:(r + 1) * ROWS], r - j * CHAINS - h) for r in range(GROUPS)])
    y[core] = ysend[core]

    lane = lax.broadcasted_iota(jnp.int32, (8, 128), 1)
    own_colour = colour_ref[0]
    packed = jnp.where(lane == 0, own_colour, me)
    for k in range(TILES):
        packed = jnp.where(lane == k + 1, tc_ref[0, k], packed)
    info[4 + pos] = packed

    pl.semaphore_wait(barrier, len(others))

    y_copy = pltpu.make_async_remote_copy(
        src_ref=ysend.at[1 - core], dst_ref=y.at[core], send_sem=y_sem.at[0], recv_sem=y_sem.at[1],
        device_id=(partner,), device_id_type=MESH)
    y_copy.start()

    def info_copy(t, slot):
        return pltpu.make_async_remote_copy(
            src_ref=info.at[4 + pos], dst_ref=info.at[slot],
            send_sem=info_send.at[t], recv_sem=info_recv.at[slot],
            device_id=(lax.rem(first + t, n),), device_id_type=MESH)

    def slot_there(t):
        group = t // 4 if isinstance(t, int) else 1
        return 4 * (2 - group) + pos

    for t in others:
        info_copy(t, slot_there(t)).start()

    def w_copy(k):
        return pltpu.make_async_remote_copy(
            src_ref=coup.at[k], dst_ref=wland.at[k], send_sem=w_send.at[k], recv_sem=w_recv.at[k],
            device_id=(partner,), device_id_type=MESH)

    def active(c):
        return jnp.where(own_colour == c, core, 1 - core)

    def out_copy(h, par, i):
        return pltpu.make_async_remote_copy(
            src_ref=xin.at[h, par, 2], dst_ref=xin.at[h, par, 2 - HOPS[i]],
            send_sem=x_send.at[h, par, i], recv_sem=x_recv.at[h, par, i],
            device_id=(chip(HOPS[i]),), device_id_type=MESH)

    def send(h, par):
        for i in range(len(HOPS)):
            out_copy(h, par, i).start()

    y_copy.wait()
    for h in range(CHAINS):
        xin[h, 0, 2] = y[active(0), h]
        send(h, 0)
    def premultiply(k, carry):
        tile_load(k).wait()
        ah, al = split(coup[k])
        left = jnp.concatenate([dsplit[0:BLOCK], dsplit[BLOCK:], dsplit[0:BLOCK]], axis=1)
        coup[k] = mm(left, jnp.concatenate([ah, ah, al], axis=0))
        w_copy(k).start()
        hi, lo = split(coup[k])
        wst[core * 7 + k, 0:BLOCK] = hi
        wst[core * 7 + k, BLOCK:] = lo
        return carry

    lax.fori_loop(0, TILES, premultiply, 0)

    for c in range(COLOURS):
        for a in range(2):
            for h in range(CHAINS):
                contrib[h, a, c] = jnp.zeros((ROWS, COLS), F32)
    wst[6] = jnp.zeros((2 * BLOCK, BLOCK), BF)
    wst[13] = jnp.zeros((2 * BLOCK, BLOCK), BF)
    keep[...] = jnp.zeros_like(keep)

    for t in others:
        info_copy(t, t).wait_recv()
        info_copy(t, slot_there(t)).wait_send()
    to_smem = pltpu.make_async_copy(info, info_smem, load_sem.at[0])
    to_smem.start()
    to_smem.wait()
    for c in range(COLOURS):
        for sl in range(3):
            where = jnp.int32(0)
            for t in range(1, 4):
                where = jnp.where(info_smem[4 * sl + t, 0, 0] == c, t, where)
            owner = first + 4 * sl + where
            owner = jnp.where(owner >= 2 * n, owner - 2 * n, jnp.where(owner >= n, owner - n, owner))
            off = 2 * (sl - 1) + jnp.where(where >= 2, 1, 0) - q + 2
            off = jnp.where(off < 0, 2, jnp.where(off > 4, 2, off))
            tab[c * 9 + sl] = off
            for a in range(2):
                index = jnp.int32(6)
                slot = 4 + 2 * q + a
                for k in range(TILES):
                    index = jnp.where(info_smem[slot, 0, k + 1] == owner, k, index)
                tab[c * 9 + 3 + 3 * a + sl] = a * 7 + index
    block_colour = [info_smem[4 + 2 * q + a, 0, 0] for a in range(2)]

    def receive_w(k, carry):
        w_copy(k).wait()
        hi, lo = split(wland[k])
        wst[(1 - core) * 7 + k, 0:BLOCK] = hi
        wst[(1 - core) * 7 + k, BLOCK:] = lo
        return carry

    lax.fori_loop(0, TILES, receive_w, 0)

    def colour_of(s):
        return jnp.where(s <= 3, s, 6 - s)

    def make_rhs(h, par, c, sl):
        near, far = jnp.maximum(2 * sl - q, 0), jnp.minimum(2 * sl - q + 1, 4)
        v = jnp.where(tab[c * 9 + sl] == near, xin[h, par, near], xin[h, par, far])
        hi = v.astype(BF).astype(F32)
        lo = v - hi
        for r in range(GROUPS):
            rows = pl.ds(pl.multiple_of(sl * BLOCK + r * ROWS, ROWS), ROWS)
            rhs[rows, 0:COLS] = jnp.where(group == r, hi, 0.0).astype(BF)
            rhs[rows, COLS:] = jnp.where(group == r, lo, 0.0).astype(BF)

    def product(c, a, slots):
        tiles = [wst[tab[c * 9 + 3 + 3 * a + sl]] for sl in slots]
        ops = [rhs[pl.ds(pl.multiple_of(sl * BLOCK, BLOCK), BLOCK)] for sl in slots]
        return mm(jnp.concatenate(tiles, axis=1), jnp.concatenate(ops, axis=0))

    def fold(v):
        v = v[0:BLOCK] + v[BLOCK:]
        v = v[:, 0:COLS] + v[:, COLS:]
        rows = [v[r * ROWS:(r + 1) * ROWS] for r in range(GROUPS)]
        total = pick(rows)
        for k in range(1, GROUPS):
            total = total + turn(pick([rows[(g - k) % GROUPS] for g in range(GROUPS)]), -k)
        return total

    def relax(h, s):
        par = lax.rem(s, 2)
        c = colour_of(s)
        nxt = active(colour_of(s + 1))
        base = y[nxt, h]
        for cc in range(COLOURS):
            base = base - jnp.where(c == cc, 0.0, contrib[h, nxt, cc])
        early, late = 2 - 2 * upper, 2 * upper

        def arrived(i):
            pltpu.make_async_remote_copy(
                src_ref=xin.at[h, par, 2], dst_ref=xin.at[h, par, 2],
                send_sem=x_send.at[h, par, i], recv_sem=x_recv.at[h, par, i],
                device_id=(partner,), device_id_type=MESH).wait_recv()

        arrived(3 - upper)
        arrived(1 - upper)

        @pl.when(jnp.logical_not(edge))
        def _():
            arrived(2 + upper)

        make_rhs(h, par, c, 1)
        make_rhs(h, par, c, early)
        acc[...] = base - fold(product(c, nxt, (1, early)))

        @pl.when(edge)
        def _():
            arrived(2 + upper)

        arrived(upper)
        make_rhs(h, par, c, late)
        value = acc[...] - fold(product(c, nxt, (late,)))
        xin[h, 1 - par, 2] = value
        tmp[...] = base - value

        @pl.when(s < EXCHANGES - 1)
        def _():
            send(h, 1 - par)

        for a in range(2):
            keep[a, h] = jnp.where(block_colour[a] == c, xin[h, par, 2], keep[a, h])

        @pl.when(s < EXCHANGES - 1)
        def _():
            other = fold(product(c, 1 - nxt, (0, 1, 2)))
            mine = tmp[...]
            contrib[h, 0, c] = jnp.where(nxt == 0, mine, other)
            contrib[h, 1, c] = jnp.where(nxt == 0, other, mine)

        for i in range(len(HOPS)):
            out_copy(h, par, i).wait_send()

    def stage(s, carry):
        for h in range(CHAINS):
            relax(h, s)
        return carry

    lax.fori_loop(0, EXCHANGES, stage, 0)

    for a in range(2):
        for h in range(CHAINS):
            keep[a, h] = jnp.where(block_colour[a] == 0, xin[h, 0, 2], keep[a, h])
    fin[core] = keep[core]
    fin_copy = pltpu.make_async_remote_copy(
        src_ref=keep.at[1 - core], dst_ref=fin.at[core], send_sem=fin_sem.at[0], recv_sem=fin_sem.at[1],
        device_id=(partner,), device_id_type=MESH)
    fin_copy.start()
    fin_copy.wait()
    for r in range(GROUPS):
        out_ref[r * ROWS:(r + 1) * ROWS] = pick(
            [turn(fin[g // CHAINS, g % CHAINS], g - r) for g in range(GROUPS)])


def per_device(n, residual, inv_diag, coupling_tiles, colour, tile_cols):
    tiles = jnp.transpose(coupling_tiles, (1, 0, 2))
    smem = pl.BlockSpec(memory_space=pltpu.SMEM)
    hbm = pl.BlockSpec(memory_space=pl.ANY)
    return pl.pallas_call(
        functools.partial(kernel, n),
        out_shape=pltpu.VMEM((BLOCK, COLS), F32),
        in_specs=[smem, smem, hbm, hbm, hbm],
        out_specs=pl.BlockSpec(memory_space=pltpu.VMEM),
        scratch_shapes=[
            pltpu.VMEM((BLOCK, COLS), F32),
            pltpu.VMEM((BLOCK, BLOCK), F32),
            pltpu.VMEM((TILES, BLOCK, BLOCK), F32),
            pltpu.VMEM((2 * BLOCK, BLOCK), BF),
            pltpu.VMEM((TILES, BLOCK, BLOCK), F32),
            pltpu.VMEM((14, 2 * BLOCK, BLOCK), BF),
            pltpu.VMEM((3 * BLOCK, 2 * COLS), BF),
            pltpu.VMEM((CHAINS, 2, 5, ROWS, COLS), F32),
            pltpu.VMEM((2, CHAINS, ROWS, COLS), F32),
            pltpu.VMEM((2, CHAINS, ROWS, COLS), F32),
            pltpu.VMEM((CHAINS, 2, COLOURS, ROWS, COLS), F32),
            pltpu.VMEM((ROWS, COLS), F32),
            pltpu.VMEM((ROWS, COLS), F32),
            pltpu.VMEM((2, CHAINS, ROWS, COLS), F32),
            pltpu.VMEM((2, CHAINS, ROWS, COLS), F32),
            pltpu.VMEM((12, 8, 128), jnp.int32),
            pltpu.SMEM((12, 8, 128), jnp.int32),
            pltpu.SMEM((9 * COLOURS,), jnp.int32),
            pltpu.SemaphoreType.DMA((2 + TILES,)),
            pltpu.SemaphoreType.DMA((12,)),
            pltpu.SemaphoreType.DMA((12,)),
            pltpu.SemaphoreType.DMA((TILES,)),
            pltpu.SemaphoreType.DMA((TILES,)),
            pltpu.SemaphoreType.DMA((2,)),
            pltpu.SemaphoreType.DMA((CHAINS, 2, len(HOPS))),
            pltpu.SemaphoreType.DMA((CHAINS, 2, len(HOPS))),
            pltpu.SemaphoreType.DMA((2,)),
        ],
        compiler_params=pltpu.CompilerParams(
            collective_id=0, has_side_effects=True, vmem_limit_bytes=56 * 1024 * 1024),
    )(colour, tile_cols, residual, inv_diag, tiles)


def solution(mesh):
    in_specs = (P("rows", None), P("rows", None), P("rows", None, None), P("rows"), P("rows", None))
    return jax.shard_map(
        functools.partial(per_device, mesh.shape["rows"]), mesh=mesh, in_specs=in_specs,
        out_specs=P("rows", None), check_vma=False)
```
